32 devices in a mesh: line: 1, freq: 4 (over z), section: 2 (over core), rcv: 4 (over y, x).
Axes of the slice: x: 2, y: 2, z: 4, core: 2. Of those that a mesh axis runs over, the one named last changes fastest.
Arguments:
- recorded: bfloat16 [512, 512, 1024], P(('line', 'freq', 'section'), 'rcv'), may hold values from -6 to 6
- signatures: bfloat16 [512, 256], P(('line', 'freq', 'section')), may hold values from -0.375 to 0.375
- ghost_delay: int32 [512, 512], P(('line', 'freq', 'section'), 'rcv'), may hold values from 8 to 47
- dead_trace: int32 [512, 512], P(('line', 'freq', 'section'), 'rcv'), may hold values 0 or 1
Outputs:
- multiples: float32 [2, 32, 512, 512], P(None, ('freq', 'section'), 'line', 'rcv')
The draws below stay inside these ranges and needn't reach their ends.
All inputs are finite; a program needn't handle non-finite values. No bound on the sum of `dead_trace` on one device may be relied on, other than what follows from the above.
Results may differ from the reference program's by a relative error of at most 0.0041.
Values may be sent and summed in bfloat16 or wider, within the bound.
No kernel may reach another device: no remote copies, remote signals or barrier semaphores. Data moves between devices by JAX's collectives and lax.ppermute only.
A program may use at most 320 MiB of HBM per device.

```python
import math
import jax
import jax.numpy as jnp
from jax import lax

STATION_COUNT = 512
SAMPLES = 1024
TAPS = 256
BINS = 32


def touch_ends(array, rng, low, top_value):
    longest = array.shape.index(max(array.shape))
    spots = []
    for shift in (0, 1):
        where = [jax.random.randint(jax.random.fold_in(rng, axis), (), 0, length) for axis, length in enumerate(array.shape)]
        where[longest] = (where[longest] + shift) % array.shape[longest]
        spots.append(tuple(where))
    return array.at[spots[0]].set(low).at[spots[1]].set(top_value)


def shard_levels(stream_key, extent, cuts, smallest, largest):
    def one(position, blocks):
        draws = jax.random.uniform(jax.random.fold_in(jax.random.fold_in(stream_key, 6), position), (blocks,), jnp.float32, smallest / len(cuts), largest / len(cuts))
        return jnp.repeat(jnp.exp(draws), extent[position] // blocks).reshape((-1,) + (1,) * (len(extent) - position - 1))

    loudness = one(*cuts[0])
    for cut in cuts[1:]:
        loudness = loudness * one(*cut)
    return loudness


def noise(stream_key, shape, spread, bound, cuts=(), kind=jnp.bfloat16):
    entries = spread * jax.random.normal(stream_key, shape, jnp.float32)
    if cuts:
        entries = entries * shard_levels(stream_key, shape, cuts, -0.22, 0.18)
    return jnp.clip(entries, -bound, bound).astype(kind)


def setup_inputs(seed: int = 0, part: int = 0) -> dict:
    keys = jax.random.split(jax.random.key(seed), 5)
    own_keys = jax.random.split(jax.random.fold_in(keys[4], part), 5)
    return {
        "recorded": noise(own_keys[0], (STATION_COUNT, STATION_COUNT, SAMPLES), 1.0, 6.0, ((0, 8), (1, 4))),
        "signatures": noise(own_keys[1], (STATION_COUNT, TAPS), TAPS ** -0.5, 0.375, ((0, 8),)),
        "ghost_delay": touch_ends(jax.random.randint(own_keys[2], (STATION_COUNT, STATION_COUNT), 8, 48), jax.random.fold_in(own_keys[2], 1), 8, 47).astype(jnp.int32),
        "dead_trace": touch_ends((jax.random.randint(own_keys[3], (STATION_COUNT, STATION_COUNT), 0, 16) < 1).astype(jnp.int32), jax.random.fold_in(own_keys[3], 1), 0, 1),
    }


reflectivity = 0.6

def ghost_gain(ghost_delay):
    bin_index = jnp.arange(1, BINS + 1, dtype=jnp.int32)
    phase_angles = (ghost_delay[..., None] * bin_index % SAMPLES).astype(jnp.float32) * (2.0 * math.pi / SAMPLES)
    cosine = jnp.cos(phase_angles)
    sine_value = jnp.sin(phase_angles)
    divisor = 1.0 - 2.0 * reflectivity * cosine + reflectivity * reflectivity
    return ((1.0 - reflectivity * cosine) / divisor, -reflectivity * sine_value / divisor)

def reference(recorded, signatures, ghost_delay, dead_trace):
    group_size = 8
    group_count = STATION_COUNT // group_size

    def one_group(group_args):
        traces, pulses, delays, deaths = group_args
        wave = traces.astype(jnp.float32)
        pulse = pulses.astype(jnp.float32)
        wavefield_spectrum = jnp.fft.rfft(wave, 2 * SAMPLES, axis=-1)
        pulse_hat = jnp.fft.rfft(pulse, 2 * SAMPLES, axis=-1)
        filtered = jnp.fft.irfft(wavefield_spectrum * pulse_hat[:, None, :], 2 * SAMPLES, axis=-1)[..., :SAMPLES]
        coeff = jnp.fft.rfft(filtered, axis=-1)[..., 1:BINS + 1] / math.sqrt(SAMPLES)
        spec_real = jnp.real(coeff)
        spec_imag = jnp.imag(coeff)
        gain_real, gain_imag = ghost_gain(delays)
        live_mask = (1 - deaths).astype(jnp.float32)[..., None]
        real_part = (spec_real * gain_real - spec_imag * gain_imag) * live_mask
        imag_part = (spec_real * gain_imag + spec_imag * gain_real) * live_mask
        stacked = jnp.stack([real_part, imag_part]).astype(jnp.bfloat16)
        return jnp.transpose(stacked, (0, 3, 1, 2))
    grouped = (recorded.reshape(group_count, group_size, STATION_COUNT, SAMPLES), signatures.reshape(group_count, group_size, TAPS), ghost_delay.reshape(group_count, group_size, STATION_COUNT), dead_trace.reshape(group_count, group_size, STATION_COUNT))
    pieces = lax.map(one_group, grouped)
    deghosted = jnp.transpose(pieces, (1, 2, 0, 3, 4)).reshape(2, BINS, STATION_COUNT, STATION_COUNT)
    factor = 1.0 / math.sqrt(STATION_COUNT)

    def one_bin(bin_pair):
        real_part = bin_pair[0].astype(jnp.float32)
        imag_part = bin_pair[1].astype(jnp.float32)
        real_out = jnp.dot(real_part, real_part, preferred_element_type=jnp.float32) - jnp.dot(imag_part, imag_part, preferred_element_type=jnp.float32)
        imag_out = jnp.dot(real_part, imag_part, preferred_element_type=jnp.float32) + jnp.dot(imag_part, real_part, preferred_element_type=jnp.float32)
        return jnp.stack([real_out, imag_out]) * factor
    multiple_model = lax.map(one_bin, jnp.transpose(deghosted, (1, 0, 2, 3)))
    return jnp.transpose(multiple_model, (1, 0, 2, 3))
```

```python
import functools
import math

import jax
import jax.numpy as jnp
import ml_dtypes
import numpy as np
from jax import lax
from jax.experimental import pallas as pl
from jax.experimental.pallas import tpu as pltpu
from jax.sharding import PartitionSpec as P

REFLECTIVITY = 0.6
LANES = 128
BLOCK = 16
SPECTRUM_VMEM = 60 * 2**20
REGROUP_VMEM = 16 * 2**20
PRODUCT_VMEM = 24 * 2**20
COLLECT_VMEM = 16 * 2**20


def split_pair(values):
    high = values.astype(ml_dtypes.bfloat16)
    low = (values - high.astype(np.float64)).astype(ml_dtypes.bfloat16)
    return high, low


@functools.lru_cache(maxsize=None)
def tables(samples, taps, bins):
    bin_index = np.arange(1, bins + 1)[:, None]
    unit = 2.0 * math.pi / samples
    time_angle = (bin_index * np.arange(samples)[None] % samples) * unit
    head = samples - taps
    factor = 1.0 / math.sqrt(samples)
    twiddle = np.concatenate([np.cos(time_angle), -np.sin(time_angle)])
    head_high, head_low = split_pair(twiddle[:, :head])
    head_table = np.concatenate([head_high, head_low])
    tap_table = (twiddle[:, :taps] * factor).astype(np.float32)
    turn_table = twiddle[:, head:].astype(np.float32)
    lane = np.arange(taps)
    prefix = (lane[:, None] <= taps - 1 - lane[None]).astype(ml_dtypes.bfloat16)
    delay_angle = (bin_index * np.arange(LANES)[None] % samples) * unit
    gain = 1.0 / (1.0 - REFLECTIVITY * np.exp(-1j * delay_angle))
    gain[:, LANES - 1] = 0.0
    gain_table = np.concatenate([gain.real, gain.imag]).astype(np.float32)
    return head_table, tap_table, turn_table, prefix, gain_table


def halves(value):
    high = value.astype(jnp.bfloat16)
    low = (value - high.astype(jnp.float32)).astype(jnp.bfloat16)
    return jnp.concatenate([high, low])


def nt_dot(left, right):
    return lax.dot_general(
        left, right, (((1,), (1,)), ((), ())), preferred_element_type=jnp.float32
    )


def spectrum_body(place, bins, head_ref, tap_ref, turn_ref, prefix_ref, gain_ref, sig_ref, delay_ref, dead_ref, rec_ref, *rest):
    out_refs, rows_ref = rest[:-1], rest[-1]
    shots, receivers, samples = rec_ref.shape
    head = head_ref.shape[1]
    both = 2 * bins
    pulses = sig_ref[...].astype(jnp.float32)
    tap_table = tap_ref[...]
    parts = [halves(tap_table * pulses[shot : shot + 1]) for shot in range(shots)]
    sums = jnp.dot(
        jnp.concatenate(parts), prefix_ref[...], preferred_element_type=jnp.float32
    )
    turn_real, turn_imag = turn_ref[:bins], turn_ref[bins:]
    traces = rec_ref[...].reshape(shots * receivers, samples)
    whole = nt_dot(head_ref[...], traces[:, :head])
    whole = whole[:both] + whole[both:]
    lookup = jnp.where(dead_ref[...] != 0, LANES - 1, delay_ref[...])
    gain_table = gain_ref[...]
    for shot in range(shots):
        base = shot * 2 * both
        filt = sums[base : base + both] + sums[base + both : base + 2 * both]
        filt_real, filt_imag = filt[:bins], filt[bins:]
        tail_filter = jnp.concatenate(
            [
                filt_real * turn_real - filt_imag * turn_imag,
                filt_real * turn_imag + filt_imag * turn_real,
            ]
        )
        columns = slice(shot * receivers, (shot + 1) * receivers)
        tail = nt_dot(halves(tail_filter), traces[columns, head:])
        tail = tail[:both] + tail[both:]
        main_real, main_imag = whole[:bins, columns], whole[bins:, columns]
        pulse_real, pulse_imag = filt_real[:, :1], filt_imag[:, :1]
        real = main_real * pulse_real - main_imag * pulse_imag + tail[:bins]
        imag = main_real * pulse_imag + main_imag * pulse_real + tail[bins:]
        index = jnp.broadcast_to(lookup[shot : shot + 1], (both, receivers))
        gain = jnp.take_along_axis(gain_table, index, axis=1)
        gain_real, gain_imag = gain[:bins], gain[bins:]
        rows_ref[:bins, shot] = real * gain_real - imag * gain_imag
        rows_ref[bins:, shot] = real * gain_imag + imag * gain_real
    place(rows_ref, out_refs)


def spectrum_call(recorded, signatures, ghost_delay, dead_trace, bins, place, out_shapes, out_specs, first, count, block):
    samples, taps, receivers = recorded.shape[2], signatures.shape[1], recorded.shape[1]
    constants = [jnp.asarray(t) for t in tables(samples, taps, bins)]
    fixed = [pl.BlockSpec(t.shape, lambda i: (0, 0), pipeline_mode=pl.Buffered(1)) for t in constants]
    start = first // block
    rows = lambda width: pl.BlockSpec((block, width), lambda i: (i + start, 0))
    return pl.pallas_call(
        functools.partial(spectrum_body, place, bins),
        grid=(count // block,),
        in_specs=fixed
        + [rows(taps), rows(receivers), rows(receivers), pl.BlockSpec((block, receivers, samples), lambda i: (i + start, 0, 0))],
        out_specs=out_specs,
        out_shape=out_shapes,
        scratch_shapes=[pltpu.VMEM((2 * bins, block, receivers), jnp.float32)],
        compiler_params=pltpu.CompilerParams(vmem_limit_bytes=SPECTRUM_VMEM),
        cost_estimate=pl.CostEstimate(flops=2 * 2 * count * receivers * samples * 4 * bins // 2, bytes_accessed=count * receivers * samples * 2, transcendentals=0),
    )(*constants, signatures, ghost_delay, dead_trace, recorded)


def split_shots(shots):
    return [(0, shots, True)]


def axis_sizes():
    return lax.axis_size("freq"), lax.axis_size("section"), lax.axis_size("rcv")


def frequency_of(deep, side, across):
    sections, groups = lax.axis_size("section"), lax.axis_size("rcv")
    return (
        (lax.axis_index("freq") ^ deep) * sections + (lax.axis_index("section") ^ side)
    ) * groups + (lax.axis_index("rcv") ^ across)


def plane_offsets():
    _, sections, groups = axis_sizes()
    return [(side, across) for side in range(sections) for across in range(groups)]


def place_plain(rows_ref, out_refs):
    (out_ref,) = out_refs
    bins = out_ref.shape[0]
    for part in range(2):
        out_ref[:, part] = rows_ref[part * bins : (part + 1) * bins].astype(out_ref.dtype)


def place_relative(plane_first, rows_ref, out_refs):
    bins = rows_ref.shape[0] // 2
    for deep in range(lax.axis_size("freq")):
        for spot, (side, across) in enumerate(plane_offsets()):
            frequency = frequency_of(deep, side, across)
            outer, inner = (spot, deep) if plane_first else (deep, spot)
            for part in range(2):
                out_refs[outer][inner, part] = rows_ref[frequency + part * bins].astype(jnp.bfloat16)


def exchange(array, offset):
    if not any(offset):
        return array
    depths, sections, groups = axis_sizes()
    deep, side, across = offset
    pairs = [
        (
            (z * sections + s) * groups + c,
            ((z ^ deep) * sections + (s ^ side)) * groups + (c ^ across),
        )
        for z in range(depths)
        for s in range(sections)
        for c in range(groups)
    ]
    return lax.ppermute(array, ("freq", "section", "rcv"), pairs)


def exchange_plane(arrays):
    return [exchange(a, (0,) + o) for a, o in zip(arrays, plane_offsets(), strict=True)]


def exchange_deep(arrays):
    return [exchange(a, (deep, 0, 0)) for deep, a in enumerate(arrays)]


def regroup_body(count, *refs):
    in_refs, out_refs = refs[:count], refs[count:]
    for outer, out_ref in enumerate(out_refs):
        for inner in range(count):
            out_ref[inner] = in_refs[inner][outer]


def in_vmem(count):
    return [pl.BlockSpec(memory_space=pltpu.VMEM)] * count


def regroup(arrays):
    count, rest = arrays[0].shape[0], arrays[0].shape[1:]
    return pl.pallas_call(
        functools.partial(regroup_body, len(arrays)),
        out_shape=[jax.ShapeDtypeStruct((len(arrays),) + rest, jnp.bfloat16)] * count,
        in_specs=in_vmem(len(arrays)),
        out_specs=in_vmem(count),
        compiler_params=pltpu.CompilerParams(vmem_limit_bytes=REGROUP_VMEM),
        cost_estimate=pl.CostEstimate(flops=0, bytes_accessed=4 * len(arrays) * arrays[0].size, transcendentals=0),
    )(*arrays)


def spectra(recorded, signatures, ghost_delay, dead_trace, first, count, plane_first):
    depths, sections, groups = axis_sizes()
    plane = sections * groups
    receivers = recorded.shape[1]
    outer, inner = (plane, depths) if plane_first else (depths, plane)
    block = min(count, BLOCK)
    return spectrum_call(
        recorded,
        signatures,
        ghost_delay,
        dead_trace,
        plane * depths,
        functools.partial(place_relative, plane_first),
        [jax.ShapeDtypeStruct((inner, 2, count, receivers), jnp.bfloat16)] * outer,
        [pl.BlockSpec((inner, 2, block, receivers), lambda i: (0, 0, i, 0))] * outer,
        first,
        count,
        block,
    )


def product_body(pieces, *refs):
    sections, groups = lax.axis_size("section"), lax.axis_size("rcv")
    left_ref = refs[-1]
    out_refs = refs[-1 - groups : -1]
    in_refs = iter(refs)
    stations = left_ref.shape[0]
    receivers = stations // groups
    my_deep, my_side, my_across = (lax.axis_index(a) for a in ("freq", "section", "rcv"))
    offsets = plane_offsets()
    shots = stations // (lax.axis_size("freq") * sections)
    for plane_last, first, count in pieces:
        outer = lax.axis_size("freq") if not plane_last else len(offsets)
        for i in range(outer):
            ref = next(in_refs)
            for j in range(ref.shape[0]):
                deep, spot = (j, i) if plane_last else (i, j)
                side, across = offsets[spot]
                row = ((my_deep ^ deep) * sections + (my_side ^ side)) * shots + first
                row = pl.multiple_of(row, math.gcd(shots, first) if first else shots)
                column = (my_across ^ across) * receivers
                for part in range(2):
                    where = pl.multiple_of(column + part * stations, receivers)
                    left_ref[pl.ds(row, count), pl.ds(where, receivers)] = ref[j, part]
    left = left_ref[...]
    scale = 1.0 / math.sqrt(stations)
    for across in range(groups):
        column = pl.multiple_of((my_across ^ across) * receivers, receivers)
        real = left_ref[:, pl.ds(column, receivers)]
        imag = left_ref[:, pl.ds(pl.multiple_of(column + stations, receivers), receivers)]
        right = jnp.concatenate(
            [jnp.concatenate([real, imag], axis=1), jnp.concatenate([-imag, real], axis=1)]
        )
        both = jnp.dot(left, right, preferred_element_type=jnp.float32) * scale
        out_ref = out_refs[across]
        out_ref[0] = both[:, :receivers].astype(out_ref.dtype)
        out_ref[1] = both[:, receivers:].astype(out_ref.dtype)


def product(arrays, pieces, stations):
    groups = lax.axis_size("rcv")
    receivers = stations // groups
    return pl.pallas_call(
        functools.partial(product_body, pieces),
        out_shape=[
            jax.ShapeDtypeStruct((2, stations, receivers), jnp.bfloat16 if across else jnp.float32)
            for across in range(groups)
        ],
        in_specs=in_vmem(len(arrays)),
        out_specs=in_vmem(groups),
        scratch_shapes=[pltpu.VMEM((stations, 2 * stations), jnp.bfloat16)],
        compiler_params=pltpu.CompilerParams(vmem_limit_bytes=PRODUCT_VMEM),
        cost_estimate=pl.CostEstimate(flops=8 * stations**3, bytes_accessed=8 * stations**2, transcendentals=0),
    )(*arrays)


def collect_body(*refs):
    in_refs, out_ref = refs[:-1], refs[-1]
    mine = lax.axis_index("rcv")
    for across, ref in enumerate(in_refs):
        for part in range(2):
            out_ref[part, mine ^ across] = ref[part].astype(out_ref.dtype)


def collect(arrays):
    parts, stations, receivers = arrays[0].shape
    return pl.pallas_call(
        collect_body,
        out_shape=jax.ShapeDtypeStruct((parts, len(arrays), stations, receivers), jnp.float32),
        in_specs=in_vmem(len(arrays)),
        out_specs=pl.BlockSpec(memory_space=pltpu.VMEM),
        compiler_params=pltpu.CompilerParams(vmem_limit_bytes=COLLECT_VMEM),
    )(*arrays)


def few_devices(recorded, signatures, ghost_delay, dead_trace):
    stations = recorded.shape[1] * lax.axis_size("rcv")
    arrays, pieces = [], []
    for first, count, plane_first in split_shots(recorded.shape[0]):
        sent = spectra(recorded, signatures, ghost_delay, dead_trace, first, count, plane_first)
        steps = (exchange_plane, exchange_deep) if plane_first else (exchange_deep, exchange_plane)
        arrays += steps[1](regroup(steps[0](sent)))
        pieces.append((not plane_first, first, count))
    blocks = product(arrays, pieces, stations)
    return collect([exchange(b, (0, 0, across)) for across, b in enumerate(blocks)])


def many_devices(recorded, signatures, ghost_delay, dead_trace):
    shots, receivers, _ = recorded.shape
    depths, sections, groups = axis_sizes()
    bins = depths * sections * groups
    block = min(shots, BLOCK)
    (deghosted,) = spectrum_call(
        recorded,
        signatures,
        ghost_delay,
        dead_trace,
        bins,
        place_plain,
        [jax.ShapeDtypeStruct((bins, 2, shots, receivers), jnp.bfloat16)],
        [pl.BlockSpec((bins, 2, block, receivers), lambda i: (0, 0, i, 0))],
        0,
        shots,
        block,
    )
    axes = ("freq", "section", "rcv")
    relayed = lax.all_to_all(deghosted, axes, split_axis=0, concat_axis=0, tiled=True)
    relayed = relayed.reshape(depths * sections, groups, 2, shots, receivers)
    stations = groups * receivers
    matrix = jnp.transpose(relayed, (2, 0, 3, 1, 4)).reshape(2, stations, stations)
    real, imag = matrix[0], matrix[1]
    dot = functools.partial(jnp.dot, preferred_element_type=jnp.float32)
    whole = jnp.stack([dot(real, real) - dot(imag, imag), dot(real, imag) + dot(imag, real)])
    whole = (whole * (1.0 / math.sqrt(stations))).astype(jnp.bfloat16)
    whole = whole.reshape(2, stations, groups, receivers)
    whole = lax.all_to_all(whole, "rcv", split_axis=2, concat_axis=0, tiled=True)
    whole = whole.reshape(groups, 2, stations, receivers)
    return jnp.transpose(whole, (1, 0, 2, 3)).astype(jnp.float32)


def per_device(recorded, signatures, ghost_delay, dead_trace):
    sizes = axis_sizes()
    small = all(n & (n - 1) == 0 for n in sizes) and sizes[0] * sizes[1] * sizes[2] <= 32
    run = few_devices if small else many_devices
    return run(recorded, signatures, ghost_delay, dead_trace)


def solution(mesh):
    return jax.shard_map(
        per_device,
        mesh=mesh,
        in_specs=(
            P(("line", "freq", "section"), "rcv", None),
            P(("line", "freq", "section"), None),
            P(("line", "freq", "section"), "rcv"),
            P(("line", "freq", "section"), "rcv"),
        ),
        out_specs=P(None, ("freq", "section"), "line", "rcv"),
        check_vma=False,
    )
```

```python
import functools
import math

import jax
import jax.numpy as jnp
import ml_dtypes
import numpy as np
from jax import lax
from jax.experimental import pallas as pl
from jax.experimental.pallas import tpu as pltpu
from jax.sharding import PartitionSpec as P

REFLECTIVITY = 0.6
LANES = 128
BLOCK = 16
SPECTRUM_VMEM = 60 * 2**20
REGROUP_VMEM = 16 * 2**20
PRODUCT_VMEM = 24 * 2**20
COLLECT_VMEM = 16 * 2**20


def split_pair(values):
    high = values.astype(ml_dtypes.bfloat16)
    low = (values - high.astype(np.float64)).astype(ml_dtypes.bfloat16)
    return high, low


@functools.lru_cache(maxsize=None)
def tables(samples, taps, bins):
    bin_index = np.arange(1, bins + 1)[:, None]
    unit = 2.0 * math.pi / samples
    time_angle = (bin_index * np.arange(samples)[None] % samples) * unit
    head = samples - taps
    factor = 1.0 / math.sqrt(samples)
    twiddle = np.concatenate([np.cos(time_angle), -np.sin(time_angle)])
    head_high, head_low = split_pair(twiddle[:, :head])
    head_table = np.concatenate([head_high, head_low])
    tap_table = (twiddle[:, :taps] * factor).astype(np.float32)
    turn_table = twiddle[:, head:].astype(np.float32)
    lane = np.arange(taps)
    prefix = (lane[:, None] <= taps - 1 - lane[None]).astype(ml_dtypes.bfloat16)
    delay_angle = (bin_index * np.arange(LANES)[None] % samples) * unit
    gain = 1.0 / (1.0 - REFLECTIVITY * np.exp(-1j * delay_angle))
    gain[:, LANES - 1] = 0.0
    gain_table = np.concatenate([gain.real, gain.imag]).astype(np.float32)
    return head_table, tap_table, turn_table, prefix, gain_table


def halves(value):
    high = value.astype(jnp.bfloat16)
    low = (value - high.astype(jnp.float32)).astype(jnp.bfloat16)
    return jnp.concatenate([high, low])


def nt_dot(left, right):
    return lax.dot_general(
        left, right, (((1,), (1,)), ((), ())), preferred_element_type=jnp.float32
    )


def spectrum_body(place, bins, head_ref, tap_ref, turn_ref, prefix_ref, gain_ref, sig_ref, delay_ref, dead_ref, rec_ref, *rest):
    out_refs, rows_ref = rest[:-1], rest[-1]
    shots, receivers, samples = rec_ref.shape
    head = head_ref.shape[1]
    both = 2 * bins
    pulses = sig_ref[...].astype(jnp.float32)
    tap_table = tap_ref[...]
    parts = [halves(tap_table * pulses[shot : shot + 1]) for shot in range(shots)]
    sums = jnp.dot(
        jnp.concatenate(parts), prefix_ref[...], preferred_element_type=jnp.float32
    )
    turn_real, turn_imag = turn_ref[:bins], turn_ref[bins:]
    traces = rec_ref[...].reshape(shots * receivers, samples)
    whole = nt_dot(head_ref[...], traces[:, :head])
    whole = whole[:both] + whole[both:]
    lookup = jnp.where(dead_ref[...] != 0, LANES - 1, delay_ref[...])
    gain_table = gain_ref[...]
    for shot in range(shots):
        base = shot * 2 * both
        filt = sums[base : base + both] + sums[base + both : base + 2 * both]
        filt_real, filt_imag = filt[:bins], filt[bins:]
        tail_filter = jnp.concatenate(
            [
                filt_real * turn_real - filt_imag * turn_imag,
                filt_real * turn_imag + filt_imag * turn_real,
            ]
        )
        columns = slice(shot * receivers, (shot + 1) * receivers)
        tail = nt_dot(halves(tail_filter), traces[columns, head:])
        tail = tail[:both] + tail[both:]
        main_real, main_imag = whole[:bins, columns], whole[bins:, columns]
        pulse_real, pulse_imag = filt_real[:, :1], filt_imag[:, :1]
        real = main_real * pulse_real - main_imag * pulse_imag + tail[:bins]
        imag = main_real * pulse_imag + main_imag * pulse_real + tail[bins:]
        index = jnp.broadcast_to(lookup[shot : shot + 1], (both, receivers))
        gain = jnp.take_along_axis(gain_table, index, axis=1)
        gain_real, gain_imag = gain[:bins], gain[bins:]
        rows_ref[:bins, shot] = real * gain_real - imag * gain_imag
        rows_ref[bins:, shot] = real * gain_imag + imag * gain_real
    place(rows_ref, out_refs)


def spectrum_call(recorded, signatures, ghost_delay, dead_trace, bins, place, out_shapes, out_specs, first, count, block):
    samples, taps, receivers = recorded.shape[2], signatures.shape[1], recorded.shape[1]
    constants = [jnp.asarray(t) for t in tables(samples, taps, bins)]
    fixed = [pl.BlockSpec(t.shape, lambda i: (0, 0), pipeline_mode=pl.Buffered(1)) for t in constants]
    start = first // block
    rows = lambda width: pl.BlockSpec((block, width), lambda i: (i + start, 0))
    return pl.pallas_call(
        functools.partial(spectrum_body, place, bins),
        grid=(count // block,),
        in_specs=fixed
        + [rows(taps), rows(receivers), rows(receivers), pl.BlockSpec((block, receivers, samples), lambda i: (i + start, 0, 0))],
        out_specs=out_specs,
        out_shape=out_shapes,
        scratch_shapes=[pltpu.VMEM((2 * bins, block, receivers), jnp.float32)],
        compiler_params=pltpu.CompilerParams(vmem_limit_bytes=SPECTRUM_VMEM),
        cost_estimate=pl.CostEstimate(flops=2 * 2 * count * receivers * samples * 4 * bins // 2, bytes_accessed=count * receivers * samples * 2, transcendentals=0),
    )(*constants, signatures, ghost_delay, dead_trace, recorded)


def axis_sizes():
    return lax.axis_size("freq"), lax.axis_size("section"), lax.axis_size("rcv")


def place_plain(rows_ref, out_refs):
    (out_ref,) = out_refs
    bins = out_ref.shape[0]
    for part in range(2):
        out_ref[:, part] = rows_ref[part * bins : (part + 1) * bins].astype(out_ref.dtype)


def exchange(array, across):
    if not across:
        return array
    return lax.ppermute(array, "rcv", [(c, c ^ across) for c in range(lax.axis_size("rcv"))])


def in_vmem(count):
    return [pl.BlockSpec(memory_space=pltpu.VMEM)] * count


def product_body(in_ref, *refs):
    groups = lax.axis_size("rcv")
    left_ref, out_refs = refs[-1], refs[:-1]
    stations = left_ref.shape[0]
    sources, _, shots, receivers = in_ref.shape
    for source in range(sources):
        rows = pl.ds(source // groups * shots, shots)
        for part in range(2):
            columns = pl.ds(source % groups * receivers + part * stations, receivers)
            left_ref[rows, columns] = in_ref[source, part]
    left = left_ref[...]
    scale = 1.0 / math.sqrt(stations)
    mine = lax.axis_index("rcv")
    for across in reversed(range(groups)):
        column = pl.multiple_of((mine ^ across) * receivers, receivers)
        real = left_ref[:, pl.ds(column, receivers)]
        imag = left_ref[:, pl.ds(pl.multiple_of(column + stations, receivers), receivers)]
        right = jnp.concatenate(
            [jnp.concatenate([real, imag], axis=1), jnp.concatenate([-imag, real], axis=1)]
        )
        both = jnp.dot(left, right, preferred_element_type=jnp.float32) * scale
        out_ref = out_refs[across]
        out_ref[0] = both[:, :receivers].astype(out_ref.dtype)
        out_ref[1] = both[:, receivers:].astype(out_ref.dtype)


def product(array):
    groups, receivers = lax.axis_size("rcv"), array.shape[3]
    stations = groups * receivers
    return pl.pallas_call(
        product_body,
        out_shape=[
            jax.ShapeDtypeStruct((2, stations, receivers), jnp.bfloat16 if across else jnp.float32)
            for across in range(groups)
        ],
        in_specs=in_vmem(1),
        out_specs=in_vmem(groups),
        scratch_shapes=[pltpu.VMEM((stations, 2 * stations), jnp.bfloat16)],
        compiler_params=pltpu.CompilerParams(vmem_limit_bytes=PRODUCT_VMEM),
        cost_estimate=pl.CostEstimate(flops=8 * stations**3, bytes_accessed=8 * stations**2, transcendentals=0),
    )(array)


def collect_body(*refs):
    in_refs, out_ref = refs[:-1], refs[-1]
    mine = lax.axis_index("rcv")
    for across, ref in enumerate(in_refs):
        for part in range(2):
            out_ref[part, mine ^ across] = ref[part].astype(out_ref.dtype)


def collect(arrays):
    parts, stations, receivers = arrays[0].shape
    return pl.pallas_call(
        collect_body,
        out_shape=jax.ShapeDtypeStruct((parts, len(arrays), stations, receivers), jnp.float32),
        in_specs=in_vmem(len(arrays)),
        out_specs=pl.BlockSpec(memory_space=pltpu.VMEM),
        compiler_params=pltpu.CompilerParams(vmem_limit_bytes=COLLECT_VMEM),
    )(*arrays)


def spectra(recorded, signatures, ghost_delay, dead_trace):
    shots, receivers, _ = recorded.shape
    bins = math.prod(axis_sizes())
    block = min(shots, BLOCK)
    (deghosted,) = spectrum_call(
        recorded,
        signatures,
        ghost_delay,
        dead_trace,
        bins,
        place_plain,
        [jax.ShapeDtypeStruct((bins, 2, shots, receivers), jnp.bfloat16)],
        [pl.BlockSpec((bins, 2, block, receivers), lambda i: (0, 0, i, 0))],
        0,
        shots,
        block,
    )
    return deghosted


def per_device(recorded, signatures, ghost_delay, dead_trace):
    deghosted = spectra(recorded, signatures, ghost_delay, dead_trace)
    axes = ("freq", "section", "rcv")
    relayed = lax.all_to_all(deghosted, axes, split_axis=0, concat_axis=0, tiled=True)
    return collect([exchange(b, across) for across, b in enumerate(product(relayed))])


def solution(mesh):
    return jax.shard_map(
        per_device,
        mesh=mesh,
        in_specs=(
            P(("line", "freq", "section"), "rcv", None),
            P(("line", "freq", "section"), None),
            P(("line", "freq", "section"), "rcv"),
            P(("line", "freq", "section"), "rcv"),
        ),
        out_specs=P(None, ("freq", "section"), "line", "rcv"),
        check_vma=False,
    )
```

```python
import functools
import math

import jax
import jax.numpy as jnp
import ml_dtypes
import numpy as np
from jax import lax
from jax.experimental import pallas as pl
from jax.experimental.pallas import tpu as pltpu
from jax.sharding import PartitionSpec as P

REFLECTIVITY = 0.6
LANES = 128
BLOCK = 16
ORDER = (3, 2, 1)
SPECTRUM_VMEM = 56 * 2**20
REGROUP_VMEM = 16 * 2**20
PRODUCT_VMEM = 24 * 2**20
COLLECT_VMEM = 16 * 2**20


def split_pair(values):
    high = values.astype(ml_dtypes.bfloat16)
    low = (values - high.astype(np.float64)).astype(ml_dtypes.bfloat16)
    return high, low


@functools.lru_cache(maxsize=None)
def tables(samples, taps, bins):
    bin_index = np.arange(1, bins + 1)[:, None]
    unit = 2.0 * math.pi / samples
    time_angle = (bin_index * np.arange(samples)[None] % samples) * unit
    head = samples - taps
    factor = 1.0 / math.sqrt(samples)
    twiddle = np.concatenate([np.cos(time_angle), -np.sin(time_angle)])
    head_high, head_low = split_pair(twiddle[:, :head])
    head_table = np.concatenate([head_high, head_low])
    tap_table = (twiddle[:, :taps] * factor).astype(np.float32)
    turn_table = twiddle[:, head:].astype(np.float32)
    lane = np.arange(taps)
    prefix = (lane[:, None] <= taps - 1 - lane[None]).astype(ml_dtypes.bfloat16)
    delay_angle = (bin_index * np.arange(LANES)[None] % samples) * unit
    gain = 1.0 / (1.0 - REFLECTIVITY * np.exp(-1j * delay_angle))
    gain[:, LANES - 1] = 0.0
    gain_table = np.concatenate([gain.real, gain.imag]).astype(np.float32)
    return head_table, tap_table, turn_table, prefix, gain_table


def halves(value):
    high = value.astype(jnp.bfloat16)
    low = (value - high.astype(jnp.float32)).astype(jnp.bfloat16)
    return jnp.concatenate([high, low])


def nt_dot(left, right):
    return lax.dot_general(
        left, right, (((1,), (1,)), ((), ())), preferred_element_type=jnp.float32
    )


def spectrum_body(bins, chunk, *refs):
    tables_count = 5
    hbm_refs, out_ref = refs[: tables_count + 4], refs[tables_count + 4]
    buffers, sems = refs[tables_count + 5 : -2], refs[-2]
    rows_ref = refs[-1]
    head_ref, tap_ref, turn_ref, prefix_ref, gain_ref, sig_ref, delay_ref, dead_ref, rec_ref = buffers
    shots, receivers, samples = rec_ref.shape
    steps = shots // chunk
    small = len(hbm_refs) - 1

    def small_copy(i):
        return pltpu.make_async_copy(hbm_refs[i], buffers[i], sems.at[i])

    def trace_copy(step):
        span = pl.ds(step * chunk, chunk)
        return pltpu.make_async_copy(hbm_refs[small].at[span], rec_ref.at[span], sems.at[small + step])

    for i in range(small):
        small_copy(i).start()
    for step in range(steps):
        trace_copy(step).start()
    for i in range(small):
        small_copy(i).wait()

    head = head_ref.shape[1]
    both = 2 * bins
    turn_real, turn_imag = turn_ref[:bins], turn_ref[bins:]

    def one_step(step, carry):
        trace_copy(step).wait()
        first = pl.multiple_of(step * chunk, chunk)
        pulses = sig_ref[pl.ds(first, chunk), :].astype(jnp.float32)
        tap_table = tap_ref[...]
        parts = [halves(tap_table * pulses[shot : shot + 1]) for shot in range(chunk)]
        sums = jnp.dot(
            jnp.concatenate(parts), prefix_ref[...], preferred_element_type=jnp.float32
        )
        span = pl.ds(first, chunk)
        lookup = jnp.where(dead_ref[span, :] != 0, LANES - 1, delay_ref[span, :])
        for shot in range(chunk):
            traces = rec_ref[first + shot]
            main = nt_dot(head_ref[...], traces[:, :head])
            main = main[:both] + main[both:]
            base = shot * 2 * both
            filt = sums[base : base + both] + sums[base + both : base + 2 * both]
            filt_real, filt_imag = filt[:bins], filt[bins:]
            tail_filter = jnp.concatenate(
                [
                    filt_real * turn_real - filt_imag * turn_imag,
                    filt_real * turn_imag + filt_imag * turn_real,
                ]
            )
            tail = nt_dot(halves(tail_filter), traces[:, head:])
            tail = tail[:both] + tail[both:]
            main_real, main_imag = main[:bins], main[bins:]
            pulse_real, pulse_imag = filt_real[:, :1], filt_imag[:, :1]
            real = main_real * pulse_real - main_imag * pulse_imag + tail[:bins]
            imag = main_real * pulse_imag + main_imag * pulse_real + tail[bins:]
            index = jnp.broadcast_to(lookup[shot : shot + 1], (both, receivers))
            gain = jnp.take_along_axis(gain_ref[...], index, axis=1)
            gain_real, gain_imag = gain[:bins], gain[bins:]
            rows_ref[:bins, shot] = real * gain_real - imag * gain_imag
            rows_ref[bins:, shot] = real * gain_imag + imag * gain_real
        for part in range(2):
            rows = rows_ref[part * bins : (part + 1) * bins]
            out_ref[:, part, span, :] = rows.astype(out_ref.dtype)
        return carry

    lax.fori_loop(0, steps, one_step, 0)


def spectra(recorded, signatures, ghost_delay, dead_trace):
    shots, receivers, samples = recorded.shape
    taps = signatures.shape[1]
    bins = math.prod(axis_sizes())
    chunk = min(shots, BLOCK)
    constants = [jnp.asarray(t) for t in tables(samples, taps, bins)]
    operands = (*constants, signatures, ghost_delay, dead_trace, recorded)
    return pl.pallas_call(
        functools.partial(spectrum_body, bins, chunk),
        in_specs=[pl.BlockSpec(memory_space=pl.ANY)] * len(operands),
        out_specs=pl.BlockSpec(memory_space=pltpu.VMEM),
        out_shape=jax.ShapeDtypeStruct((bins, 2, shots, receivers), jnp.bfloat16),
        scratch_shapes=[pltpu.VMEM(x.shape, x.dtype) for x in operands]
        + [
            pltpu.SemaphoreType.DMA((len(operands) - 1 + shots // chunk,)),
            pltpu.VMEM((2 * bins, chunk, receivers), jnp.float32),
        ],
        compiler_params=pltpu.CompilerParams(vmem_limit_bytes=SPECTRUM_VMEM),
        cost_estimate=pl.CostEstimate(
            flops=8 * bins * recorded.size, bytes_accessed=2 * recorded.size, transcendentals=0
        ),
    )(*operands)


def axis_sizes():
    return lax.axis_size("freq"), lax.axis_size("section"), lax.axis_size("rcv")


def exchange(array, across):
    if not across:
        return array
    return lax.ppermute(array, "rcv", [(c, c ^ across) for c in range(lax.axis_size("rcv"))])


def in_vmem(count):
    return [pl.BlockSpec(memory_space=pltpu.VMEM)] * count


def own_columns(part_ref, across):
    stations = part_ref.shape[0]
    receivers = stations // lax.axis_size("rcv")
    column = (lax.axis_index("rcv") ^ across) * receivers
    return part_ref[:, pl.ds(pl.multiple_of(column, receivers), receivers)]


def block_product(real_ref, imag_ref, across):
    stations = real_ref.shape[0]
    real, imag = own_columns(real_ref, across), own_columns(imag_ref, across)
    right = jnp.concatenate(
        [jnp.concatenate([real, imag], axis=1), jnp.concatenate([-imag, real], axis=1)]
    )
    left = jnp.concatenate([real_ref[...], imag_ref[...]], axis=1)
    both = jnp.dot(left, right, preferred_element_type=jnp.float32)
    both = both * (1.0 / math.sqrt(stations))
    receivers = real.shape[1]
    return both[:, :receivers], both[:, receivers:]


def first_product_body(in_ref, real_ref, imag_ref, out_ref):
    groups = lax.axis_size("rcv")
    sources, _, shots, receivers = in_ref.shape
    for source in range(sources):
        rows = pl.ds(source // groups * shots, shots)
        columns = pl.ds(source % groups * receivers, receivers)
        real_ref[rows, columns] = in_ref[source, 0]
        imag_ref[rows, columns] = in_ref[source, 1]
    for part, block in enumerate(block_product(real_ref, imag_ref, ORDER[0])):
        out_ref[part] = block.astype(out_ref.dtype)


def other_product_body(real_ref, imag_ref, *out_refs):
    for across, out_ref in zip(ORDER[1:], out_refs, strict=True):
        for part, block in enumerate(block_product(real_ref, imag_ref, across)):
            out_ref[part] = block.astype(out_ref.dtype)


def own_product_body(real_ref, imag_ref, result_ref, own_ref, sems):
    mine = lax.axis_index("rcv")
    copies = []
    for part, block in enumerate(block_product(real_ref, imag_ref, 0)):
        own_ref[part] = block
        copy = pltpu.make_async_copy(
            own_ref.at[part], result_ref.at[part, mine], sems.at[part]
        )
        copy.start()
        copies.append(copy)
    for copy in copies:
        copy.wait()


def collect_body(offsets, *refs):
    in_refs, (result_ref, wide_ref, sems) = refs[: len(offsets)], refs[-3:]
    mine = lax.axis_index("rcv")
    copies = []
    for i, (across, in_ref) in enumerate(zip(offsets, in_refs, strict=True)):
        for part in range(2):
            wide_ref[i, part] = in_ref[part].astype(jnp.float32)
            copy = pltpu.make_async_copy(
                wide_ref.at[i, part], result_ref.at[part, mine ^ across], sems.at[i, part]
            )
            copy.start()
            copies.append(copy)
    for copy in copies:
        copy.wait()


def collect(arrays, offsets, result):
    anywhere = pl.BlockSpec(memory_space=pl.ANY)
    count, size = len(arrays), arrays[0].size
    return pl.pallas_call(
        functools.partial(collect_body, offsets),
        out_shape=jax.ShapeDtypeStruct(result.shape, result.dtype),
        in_specs=in_vmem(count) + [anywhere],
        out_specs=anywhere,
        scratch_shapes=[
            pltpu.VMEM((count,) + arrays[0].shape, jnp.float32),
            pltpu.SemaphoreType.DMA((count, 2)),
        ],
        input_output_aliases={count: 0},
        compiler_params=pltpu.CompilerParams(vmem_limit_bytes=COLLECT_VMEM),
        cost_estimate=pl.CostEstimate(flops=0, bytes_accessed=6 * count * size, transcendentals=0),
    )(*arrays, result)


def products(array):
    groups, receivers = lax.axis_size("rcv"), array.shape[3]
    stations = groups * receivers
    matrix = jax.ShapeDtypeStruct((stations, stations), jnp.bfloat16)
    block = jax.ShapeDtypeStruct((2, stations, receivers), jnp.bfloat16)

    def options(count):
        return {
            "compiler_params": pltpu.CompilerParams(vmem_limit_bytes=PRODUCT_VMEM),
            "cost_estimate": pl.CostEstimate(
                flops=8 * count * stations**2 * receivers,
                bytes_accessed=4 * stations**2,
                transcendentals=0,
            ),
        }

    real, imag, first = pl.pallas_call(
        first_product_body,
        out_shape=[matrix, matrix, block],
        in_specs=in_vmem(1),
        out_specs=in_vmem(3),
        **options(1),
    )(array)
    others = pl.pallas_call(
        other_product_body,
        out_shape=[block] * (groups - 2),
        in_specs=in_vmem(2),
        out_specs=in_vmem(groups - 2),
        **options(groups - 2),
    )(real, imag)
    own = pl.pallas_call(
        own_product_body,
        out_shape=jax.ShapeDtypeStruct((2, groups, stations, receivers), jnp.float32),
        in_specs=in_vmem(2),
        out_specs=pl.BlockSpec(memory_space=pl.ANY),
        scratch_shapes=[
            pltpu.VMEM((2, stations, receivers), jnp.float32),
            pltpu.SemaphoreType.DMA((2,)),
        ],
        **options(1),
    )(real, imag)
    return [first, *others], own


def per_device(recorded, signatures, ghost_delay, dead_trace):
    deghosted = spectra(recorded, signatures, ghost_delay, dead_trace)
    axes = ("freq", "section", "rcv")
    relayed = lax.all_to_all(deghosted, axes, split_axis=0, concat_axis=0, tiled=True)
    blocks, result = products(relayed)
    arrived = [exchange(block, across) for across, block in zip(ORDER, blocks, strict=True)]
    result = collect(arrived[:1], ORDER[:1], result)
    return collect(arrived[1:], ORDER[1:], result)


def solution(mesh):
    return jax.shard_map(
        per_device,
        mesh=mesh,
        in_specs=(
            P(("line", "freq", "section"), "rcv", None),
            P(("line", "freq", "section"), None),
            P(("line", "freq", "section"), "rcv"),
            P(("line", "freq", "section"), "rcv"),
        ),
        out_specs=P(None, ("freq", "section"), "line", "rcv"),
        check_vma=False,
    )
```

```python
import functools
import math

import jax
import jax.numpy as jnp
import ml_dtypes
import numpy as np
from jax import lax
from jax.experimental import pallas as pl
from jax.experimental.pallas import tpu as pltpu
from jax.sharding import PartitionSpec as P

REFLECTIVITY = 0.6
LANES = 128
BLOCK = 16
STEPS = ((1, 2), (3, 3), (2, 1))
SPECTRUM_VMEM = 56 * 2**20
REGROUP_VMEM = 16 * 2**20
PRODUCT_VMEM = 24 * 2**20
COLLECT_VMEM = 16 * 2**20


def split_pair(values):
    high = values.astype(ml_dtypes.bfloat16)
    low = (values - high.astype(np.float64)).astype(ml_dtypes.bfloat16)
    return high, low


@functools.lru_cache(maxsize=None)
def tables(samples, taps, bins):
    bin_index = np.arange(1, bins + 1)[:, None]
    unit = 2.0 * math.pi / samples
    time_angle = (bin_index * np.arange(samples)[None] % samples) * unit
    head = samples - taps
    factor = 1.0 / math.sqrt(samples)
    twiddle = np.concatenate([np.cos(time_angle), -np.sin(time_angle)])
    head_high, head_low = split_pair(twiddle[:, :head])
    head_table = np.concatenate([head_high, head_low])
    tap_table = (twiddle[:, :taps] * factor).astype(np.float32)
    turn_table = twiddle[:, head:].astype(np.float32)
    lane = np.arange(taps)
    prefix = (lane[:, None] <= taps - 1 - lane[None]).astype(ml_dtypes.bfloat16)
    delay_angle = (bin_index * np.arange(LANES)[None] % samples) * unit
    gain = 1.0 / (1.0 - REFLECTIVITY * np.exp(-1j * delay_angle))
    gain[:, LANES - 1] = 0.0
    gain_table = np.concatenate([gain.real, gain.imag]).astype(np.float32)
    return head_table, tap_table, turn_table, prefix, gain_table


def halves(value):
    high = value.astype(jnp.bfloat16)
    low = (value - high.astype(jnp.float32)).astype(jnp.bfloat16)
    return jnp.concatenate([high, low])


def nt_dot(left, right):
    return lax.dot_general(
        left, right, (((1,), (1,)), ((), ())), preferred_element_type=jnp.float32
    )


def spectrum_body(bins, chunk, *refs):
    tables_count = 5
    hbm_refs, out_ref = refs[: tables_count + 4], refs[tables_count + 4]
    buffers, sems = refs[tables_count + 5 : -2], refs[-2]
    rows_ref = refs[-1]
    head_ref, tap_ref, turn_ref, prefix_ref, gain_ref, sig_ref, delay_ref, dead_ref, rec_ref = buffers
    shots, receivers, samples = rec_ref.shape
    steps = shots // chunk
    small = len(hbm_refs) - 1

    def small_copy(i):
        return pltpu.make_async_copy(hbm_refs[i], buffers[i], sems.at[i])

    def trace_copy(step):
        span = pl.ds(step * chunk, chunk)
        return pltpu.make_async_copy(hbm_refs[small].at[span], rec_ref.at[span], sems.at[small + step])

    for i in range(small):
        small_copy(i).start()
    for step in range(steps):
        trace_copy(step).start()
    for i in range(small):
        small_copy(i).wait()

    head = head_ref.shape[1]
    both = 2 * bins
    turn_real, turn_imag = turn_ref[:bins], turn_ref[bins:]

    def one_step(step, carry):
        trace_copy(step).wait()
        first = pl.multiple_of(step * chunk, chunk)
        pulses = sig_ref[pl.ds(first, chunk), :].astype(jnp.float32)
        tap_table = tap_ref[...]
        parts = [halves(tap_table * pulses[shot : shot + 1]) for shot in range(chunk)]
        sums = jnp.dot(
            jnp.concatenate(parts), prefix_ref[...], preferred_element_type=jnp.float32
        )
        span = pl.ds(first, chunk)
        lookup = jnp.where(dead_ref[span, :] != 0, LANES - 1, delay_ref[span, :])
        for shot in range(chunk):
            traces = rec_ref[first + shot]
            main = nt_dot(head_ref[...], traces[:, :head])
            main = main[:both] + main[both:]
            base = shot * 2 * both
            filt = sums[base : base + both] + sums[base + both : base + 2 * both]
            filt_real, filt_imag = filt[:bins], filt[bins:]
            tail_filter = jnp.concatenate(
                [
                    filt_real * turn_real - filt_imag * turn_imag,
                    filt_real * turn_imag + filt_imag * turn_real,
                ]
            )
            tail = nt_dot(halves(tail_filter), traces[:, head:])
            tail = tail[:both] + tail[both:]
            main_real, main_imag = main[:bins], main[bins:]
            pulse_real, pulse_imag = filt_real[:, :1], filt_imag[:, :1]
            real = main_real * pulse_real - main_imag * pulse_imag + tail[:bins]
            imag = main_real * pulse_imag + main_imag * pulse_real + tail[bins:]
            index = jnp.broadcast_to(lookup[shot : shot + 1], (both, receivers))
            gain = jnp.take_along_axis(gain_ref[...], index, axis=1)
            gain_real, gain_imag = gain[:bins], gain[bins:]
            rows_ref[:bins, shot] = real * gain_real - imag * gain_imag
            rows_ref[bins:, shot] = real * gain_imag + imag * gain_real
        for part in range(2):
            rows = rows_ref[part * bins : (part + 1) * bins]
            out_ref[:, part, span, :] = rows.astype(out_ref.dtype)
        return carry

    lax.fori_loop(0, steps, one_step, 0)


def spectra(recorded, signatures, ghost_delay, dead_trace):
    shots, receivers, samples = recorded.shape
    taps = signatures.shape[1]
    bins = math.prod(axis_sizes())
    chunk = min(shots, BLOCK)
    constants = [jnp.asarray(t) for t in tables(samples, taps, bins)]
    operands = (*constants, signatures, ghost_delay, dead_trace, recorded)
    return pl.pallas_call(
        functools.partial(spectrum_body, bins, chunk),
        in_specs=[pl.BlockSpec(memory_space=pltpu.HBM)] * len(operands),
        out_specs=pl.BlockSpec(memory_space=pltpu.VMEM),
        out_shape=jax.ShapeDtypeStruct((bins, 2, shots, receivers), jnp.bfloat16),
        scratch_shapes=[pltpu.VMEM(x.shape, x.dtype) for x in operands]
        + [
            pltpu.SemaphoreType.DMA((len(operands) - 1 + shots // chunk,)),
            pltpu.VMEM((2 * bins, chunk, receivers), jnp.float32),
        ],
        compiler_params=pltpu.CompilerParams(vmem_limit_bytes=SPECTRUM_VMEM),
        cost_estimate=pl.CostEstimate(
            flops=8 * bins * recorded.size, bytes_accessed=2 * recorded.size, transcendentals=0
        ),
    )(*operands)


def axis_sizes():
    return lax.axis_size("freq"), lax.axis_size("section"), lax.axis_size("rcv")


def exchange(array, step):
    sections, groups = lax.axis_size("section"), lax.axis_size("rcv")
    pairs = [
        (s * groups + c, s * groups + (c ^ STEPS[step][s % 2]))
        for s in range(sections)
        for c in range(groups)
    ]
    return lax.ppermute(array, ("section", "rcv"), pairs)


def partner(step):
    even, odd = STEPS[step]
    return lax.axis_index("rcv") ^ jnp.where(lax.axis_index("section") % 2 == 0, even, odd)


def in_vmem(count):
    return [pl.BlockSpec(memory_space=pltpu.VMEM)] * count


def group_columns(part_ref, group):
    receivers = part_ref.shape[0] // lax.axis_size("rcv")
    return part_ref[:, pl.ds(pl.multiple_of(group * receivers, receivers), receivers)]


def block_product(real_ref, imag_ref, group):
    stations = real_ref.shape[0]
    real, imag = group_columns(real_ref, group), group_columns(imag_ref, group)
    right = jnp.concatenate(
        [jnp.concatenate([real, imag], axis=1), jnp.concatenate([-imag, real], axis=1)]
    )
    left = jnp.concatenate([real_ref[...], imag_ref[...]], axis=1)
    both = jnp.dot(left, right, preferred_element_type=jnp.float32)
    both = both * (1.0 / math.sqrt(stations))
    receivers = real.shape[1]
    return both[:, :receivers], both[:, receivers:]


def first_product_body(in_ref, real_ref, imag_ref, out_ref):
    groups = lax.axis_size("rcv")
    sources, _, shots, receivers = in_ref.shape
    for source in range(sources):
        rows = pl.ds(source // groups * shots, shots)
        columns = pl.ds(source % groups * receivers, receivers)
        real_ref[rows, columns] = in_ref[source, 0]
        imag_ref[rows, columns] = in_ref[source, 1]
    for part, block in enumerate(block_product(real_ref, imag_ref, partner(0))):
        out_ref[part] = block.astype(out_ref.dtype)


def other_product_body(real_ref, imag_ref, *out_refs):
    for step, out_ref in enumerate(out_refs, 1):
        for part, block in enumerate(block_product(real_ref, imag_ref, partner(step))):
            out_ref[part] = block.astype(out_ref.dtype)


def own_product_body(real_ref, imag_ref, result_ref, own_ref, sems):
    mine = lax.axis_index("rcv")
    copies = []
    for part, block in enumerate(block_product(real_ref, imag_ref, mine)):
        own_ref[part] = block
        copy = pltpu.make_async_copy(
            own_ref.at[part], result_ref.at[part, mine], sems.at[part]
        )
        copy.start()
        copies.append(copy)
    for copy in copies:
        copy.wait()


def collect_body(steps, *refs):
    in_refs, (result_ref, wide_ref, sems) = refs[: len(steps)], refs[-3:]
    copies = []
    for i, (step, in_ref) in enumerate(zip(steps, in_refs, strict=True)):
        for part in range(2):
            wide_ref[i, part] = in_ref[part].astype(jnp.float32)
            copy = pltpu.make_async_copy(
                wide_ref.at[i, part], result_ref.at[part, partner(step)], sems.at[i, part]
            )
            copy.start()
            copies.append(copy)
    for copy in copies:
        copy.wait()


def collect(arrays, steps, result):
    anywhere = pl.BlockSpec(memory_space=pl.ANY)
    count, size = len(arrays), arrays[0].size
    return pl.pallas_call(
        functools.partial(collect_body, steps),
        out_shape=jax.ShapeDtypeStruct(result.shape, result.dtype),
        in_specs=in_vmem(count) + [anywhere],
        out_specs=anywhere,
        scratch_shapes=[
            pltpu.VMEM((count,) + arrays[0].shape, jnp.float32),
            pltpu.SemaphoreType.DMA((count, 2)),
        ],
        input_output_aliases={count: 0},
        compiler_params=pltpu.CompilerParams(vmem_limit_bytes=COLLECT_VMEM),
        cost_estimate=pl.CostEstimate(flops=0, bytes_accessed=6 * count * size, transcendentals=0),
    )(*arrays, result)


def products(array):
    groups, receivers = lax.axis_size("rcv"), array.shape[3]
    stations = groups * receivers
    matrix = jax.ShapeDtypeStruct((stations, stations), jnp.bfloat16)
    block = jax.ShapeDtypeStruct((2, stations, receivers), jnp.bfloat16)

    def options(count):
        return {
            "compiler_params": pltpu.CompilerParams(vmem_limit_bytes=PRODUCT_VMEM),
            "cost_estimate": pl.CostEstimate(
                flops=8 * count * stations**2 * receivers,
                bytes_accessed=4 * stations**2,
                transcendentals=0,
            ),
        }

    real, imag, first = pl.pallas_call(
        first_product_body,
        out_shape=[matrix, matrix, block],
        in_specs=in_vmem(1),
        out_specs=in_vmem(3),
        **options(1),
    )(array)
    others = pl.pallas_call(
        other_product_body,
        out_shape=[block] * (groups - 2),
        in_specs=in_vmem(2),
        out_specs=in_vmem(groups - 2),
        **options(groups - 2),
    )(real, imag)
    own = pl.pallas_call(
        own_product_body,
        out_shape=jax.ShapeDtypeStruct((2, groups, stations, receivers), jnp.float32),
        in_specs=in_vmem(2),
        out_specs=pl.BlockSpec(memory_space=pl.ANY),
        scratch_shapes=[
            pltpu.VMEM((2, stations, receivers), jnp.float32),
            pltpu.SemaphoreType.DMA((2,)),
        ],
        **options(1),
    )(real, imag)
    return [first, *others], own


def per_device(recorded, signatures, ghost_delay, dead_trace):
    deghosted = spectra(recorded, signatures, ghost_delay, dead_trace)
    axes = ("freq", "section", "rcv")
    relayed = lax.all_to_all(deghosted, axes, split_axis=0, concat_axis=0, tiled=True)
    blocks, result = products(relayed)
    arrived = [exchange(block, step) for step, block in enumerate(blocks)]
    result = collect(arrived[:1], (0,), result)
    return collect(arrived[1:], (1, 2), result)


def solution(mesh):
    return jax.shard_map(
        per_device,
        mesh=mesh,
        in_specs=(
            P(("line", "freq", "section"), "rcv", None),
            P(("line", "freq", "section"), None),
            P(("line", "freq", "section"), "rcv"),
            P(("line", "freq", "section"), "rcv"),
        ),
        out_specs=P(None, ("freq", "section"), "line", "rcv"),
        check_vma=False,
    )
```

```python
import functools
import math

import jax
import jax.numpy as jnp
import ml_dtypes
import numpy as np
from jax import lax
from jax.experimental import pallas as pl
from jax.experimental.pallas import tpu as pltpu
from jax.sharding import PartitionSpec as P

REFLECTIVITY = 0.6
LANES = 128
BLOCK = 16
STEPS = ((1, 2), (3, 3), (2, 1))
SPECTRUM_VMEM = 56 * 2**20
REGROUP_VMEM = 16 * 2**20
PRODUCT_VMEM = 24 * 2**20
COLLECT_VMEM = 16 * 2**20


def split_pair(values):
    high = values.astype(ml_dtypes.bfloat16)
    low = (values - high.astype(np.float64)).astype(ml_dtypes.bfloat16)
    return high, low


@functools.lru_cache(maxsize=None)
def tables(samples, taps, bins):
    bin_index = np.arange(1, bins + 1)[:, None]
    unit = 2.0 * math.pi / samples
    time_angle = (bin_index * np.arange(samples)[None] % samples) * unit
    head = samples - taps
    factor = 1.0 / math.sqrt(samples)
    twiddle = np.concatenate([np.cos(time_angle), -np.sin(time_angle)])
    head_high, head_low = split_pair(twiddle[:, :head])
    head_table = np.concatenate([head_high, head_low])
    tap_table = (twiddle[:, :taps] * factor).astype(np.float32)
    turn_table = twiddle[:, head:].astype(np.float32)
    lane = np.arange(taps)
    prefix = (lane[:, None] <= taps - 1 - lane[None]).astype(ml_dtypes.bfloat16)
    delay_angle = (bin_index * np.arange(LANES)[None] % samples) * unit
    gain = 1.0 / (1.0 - REFLECTIVITY * np.exp(-1j * delay_angle))
    gain[:, LANES - 1] = 0.0
    gain_table = np.concatenate([gain.real, gain.imag]).astype(np.float32)
    return head_table, tap_table, turn_table, prefix, gain_table


def halves(value):
    high = value.astype(jnp.bfloat16)
    low = (value - high.astype(jnp.float32)).astype(jnp.bfloat16)
    return jnp.concatenate([high, low])


def nt_dot(left, right):
    return lax.dot_general(
        left, right, (((1,), (1,)), ((), ())), preferred_element_type=jnp.float32
    )


def spectrum_body(bins, chunk, *refs):
    tables_count = 5
    hbm_refs, out_ref = refs[: tables_count + 4], refs[tables_count + 4]
    buffers, sems = refs[tables_count + 5 : -2], refs[-2]
    rows_ref = refs[-1]
    head_ref, tap_ref, turn_ref, prefix_ref, gain_ref, sig_ref, delay_ref, dead_ref, rec_ref = buffers
    shots, receivers, samples = rec_ref.shape
    steps = shots // chunk
    small = len(hbm_refs) - 1

    def small_copy(i):
        return pltpu.make_async_copy(hbm_refs[i], buffers[i], sems.at[i])

    def trace_copy(step):
        span = pl.ds(step * chunk, chunk)
        return pltpu.make_async_copy(hbm_refs[small].at[span], rec_ref.at[span], sems.at[small + step])

    for i in range(small):
        small_copy(i).start()
    for step in range(steps):
        trace_copy(step).start()
    for i in range(small):
        small_copy(i).wait()

    head = head_ref.shape[1]
    both = 2 * bins
    turn_real, turn_imag = turn_ref[:bins], turn_ref[bins:]

    def one_step(step, carry):
        trace_copy(step).wait()
        first = pl.multiple_of(step * chunk, chunk)
        pulses = sig_ref[pl.ds(first, chunk), :].astype(jnp.float32)
        tap_table = tap_ref[...]
        parts = [halves(tap_table * pulses[shot : shot + 1]) for shot in range(chunk)]
        sums = jnp.dot(
            jnp.concatenate(parts), prefix_ref[...], preferred_element_type=jnp.float32
        )
        span = pl.ds(first, chunk)
        lookup = jnp.where(dead_ref[span, :] != 0, LANES - 1, delay_ref[span, :])
        for shot in range(chunk):
            traces = rec_ref[first + shot]
            main = nt_dot(head_ref[...], traces[:, :head])
            main = main[:both] + main[both:]
            base = shot * 2 * both
            filt = sums[base : base + both] + sums[base + both : base + 2 * both]
            filt_real, filt_imag = filt[:bins], filt[bins:]
            tail_filter = jnp.concatenate(
                [
                    filt_real * turn_real - filt_imag * turn_imag,
                    filt_real * turn_imag + filt_imag * turn_real,
                ]
            )
            tail = nt_dot(halves(tail_filter), traces[:, head:])
            tail = tail[:both] + tail[both:]
            main_real, main_imag = main[:bins], main[bins:]
            pulse_real, pulse_imag = filt_real[:, :1], filt_imag[:, :1]
            real = main_real * pulse_real - main_imag * pulse_imag + tail[:bins]
            imag = main_real * pulse_imag + main_imag * pulse_real + tail[bins:]
            index = jnp.broadcast_to(lookup[shot : shot + 1], (both, receivers))
            gain = jnp.take_along_axis(gain_ref[...], index, axis=1)
            gain_real, gain_imag = gain[:bins], gain[bins:]
            rows_ref[:bins, shot] = real * gain_real - imag * gain_imag
            rows_ref[bins:, shot] = real * gain_imag + imag * gain_real
        for part in range(2):
            rows = rows_ref[part * bins : (part + 1) * bins]
            out_ref[:, part, span, :] = rows.astype(out_ref.dtype)
        return carry

    lax.fori_loop(0, steps, one_step, 0)


def spectra(recorded, signatures, ghost_delay, dead_trace):
    shots, receivers, samples = recorded.shape
    taps = signatures.shape[1]
    bins = math.prod(axis_sizes())
    chunk = min(shots, BLOCK)
    constants = [jnp.asarray(t) for t in tables(samples, taps, bins)]
    operands = (*constants, signatures, ghost_delay, dead_trace, recorded)
    return pl.pallas_call(
        functools.partial(spectrum_body, bins, chunk),
        in_specs=[pl.BlockSpec(memory_space=pltpu.HBM)] * len(operands),
        out_specs=pl.BlockSpec(memory_space=pltpu.VMEM),
        out_shape=jax.ShapeDtypeStruct((bins, 2, shots, receivers), jnp.bfloat16),
        scratch_shapes=[pltpu.VMEM(x.shape, x.dtype) for x in operands]
        + [
            pltpu.SemaphoreType.DMA((len(operands) - 1 + shots // chunk,)),
            pltpu.VMEM((2 * bins, chunk, receivers), jnp.float32),
        ],
        compiler_params=pltpu.CompilerParams(vmem_limit_bytes=SPECTRUM_VMEM),
        cost_estimate=pl.CostEstimate(
            flops=8 * bins * recorded.size, bytes_accessed=2 * recorded.size, transcendentals=0
        ),
    )(*operands)


def axis_sizes():
    return lax.axis_size("freq"), lax.axis_size("section"), lax.axis_size("rcv")


def exchange(array, step):
    sections, groups = lax.axis_size("section"), lax.axis_size("rcv")
    pairs = [
        (s * groups + c, s * groups + (c ^ STEPS[step][s % 2]))
        for s in range(sections)
        for c in range(groups)
    ]
    return lax.ppermute(array, ("section", "rcv"), pairs)


def partner(step):
    even, odd = STEPS[step]
    return lax.axis_index("rcv") ^ jnp.where(lax.axis_index("section") % 2 == 0, even, odd)


def in_vmem(count):
    return [pl.BlockSpec(memory_space=pltpu.VMEM)] * count


def group_columns(part_ref, group):
    receivers = part_ref.shape[0] // lax.axis_size("rcv")
    return part_ref[:, pl.ds(pl.multiple_of(group * receivers, receivers), receivers)]


def block_product(real_ref, imag_ref, group):
    stations = real_ref.shape[0]
    real, imag = group_columns(real_ref, group), group_columns(imag_ref, group)
    right = jnp.concatenate(
        [jnp.concatenate([real, imag], axis=1), jnp.concatenate([-imag, real], axis=1)]
    )
    left = jnp.concatenate([real_ref[...], imag_ref[...]], axis=1)
    both = jnp.dot(left, right, preferred_element_type=jnp.float32)
    both = both * (1.0 / math.sqrt(stations))
    receivers = real.shape[1]
    return both[:, :receivers], both[:, receivers:]


def first_product_body(in_ref, real_ref, imag_ref, out_ref):
    groups = lax.axis_size("rcv")
    sources, _, shots, receivers = in_ref.shape
    for source in range(sources):
        rows = pl.ds(source // groups * shots, shots)
        columns = pl.ds(source % groups * receivers, receivers)
        real_ref[rows, columns] = in_ref[source, 0]
        imag_ref[rows, columns] = in_ref[source, 1]
    for part, block in enumerate(block_product(real_ref, imag_ref, partner(0))):
        out_ref[part] = block.astype(out_ref.dtype)


def other_product_body(real_ref, imag_ref, *out_refs):
    for step, out_ref in enumerate(out_refs, 1):
        for part, block in enumerate(block_product(real_ref, imag_ref, partner(step))):
            out_ref[part] = block.astype(out_ref.dtype)


def own_product_body(real_ref, imag_ref, result_ref, own_ref, sems):
    mine = lax.axis_index("rcv")
    copies = []
    for part, block in enumerate(block_product(real_ref, imag_ref, mine)):
        own_ref[part] = block
        copy = pltpu.make_async_copy(
            own_ref.at[part], result_ref.at[part, mine], sems.at[part]
        )
        copy.start()
        copies.append(copy)
    for copy in copies:
        copy.wait()


def collect_body(steps, *refs):
    in_refs, (result_ref, wide_ref, sems) = refs[: len(steps)], refs[-3:]
    copies = []
    for i, (step, in_ref) in enumerate(zip(steps, in_refs, strict=True)):
        for part in range(2):
            wide_ref[i, part] = in_ref[part].astype(jnp.float32)
            copy = pltpu.make_async_copy(
                wide_ref.at[i, part], result_ref.at[part, partner(step)], sems.at[i, part]
            )
            copy.start()
            copies.append(copy)
    for copy in copies:
        copy.wait()


def collect(arrays, steps, result):
    anywhere = pl.BlockSpec(memory_space=pl.ANY)
    count, size = len(arrays), arrays[0].size
    return pl.pallas_call(
        functools.partial(collect_body, steps),
        out_shape=jax.ShapeDtypeStruct(result.shape, result.dtype),
        in_specs=in_vmem(count) + [anywhere],
        out_specs=anywhere,
        scratch_shapes=[
            pltpu.VMEM((count,) + arrays[0].shape, jnp.float32),
            pltpu.SemaphoreType.DMA((count, 2)),
        ],
        input_output_aliases={count: 0},
        compiler_params=pltpu.CompilerParams(vmem_limit_bytes=COLLECT_VMEM),
        cost_estimate=pl.CostEstimate(flops=0, bytes_accessed=6 * count * size, transcendentals=0),
    )(*arrays, result)


def products(array):
    groups, receivers = lax.axis_size("rcv"), array.shape[3]
    stations = groups * receivers
    matrix = jax.ShapeDtypeStruct((stations, stations), jnp.bfloat16)
    block = jax.ShapeDtypeStruct((2, stations, receivers), jnp.bfloat16)

    def options(count):
        return {
            "compiler_params": pltpu.CompilerParams(vmem_limit_bytes=PRODUCT_VMEM),
            "cost_estimate": pl.CostEstimate(
                flops=8 * count * stations**2 * receivers,
                bytes_accessed=4 * stations**2,
                transcendentals=0,
            ),
        }

    real, imag, first = pl.pallas_call(
        first_product_body,
        out_shape=[matrix, matrix, block],
        in_specs=in_vmem(1),
        out_specs=in_vmem(3),
        **options(1),
    )(array)
    others = pl.pallas_call(
        other_product_body,
        out_shape=[block] * (groups - 2),
        in_specs=in_vmem(2),
        out_specs=in_vmem(groups - 2),
        **options(groups - 2),
    )(real, imag)
    own = pl.pallas_call(
        own_product_body,
        out_shape=jax.ShapeDtypeStruct((2, groups, stations, receivers), jnp.float32),
        in_specs=in_vmem(2),
        out_specs=pl.BlockSpec(memory_space=pl.ANY),
        scratch_shapes=[
            pltpu.VMEM((2, stations, receivers), jnp.float32),
            pltpu.SemaphoreType.DMA((2,)),
        ],
        **options(1),
    )(real, imag)
    return [first, *others], own


def per_device(recorded, signatures, ghost_delay, dead_trace):
    deghosted = spectra(recorded, signatures, ghost_delay, dead_trace)
    axes = ("freq", "section", "rcv")
    relayed = lax.all_to_all(deghosted, axes, split_axis=0, concat_axis=0, tiled=True)
    blocks, result = products(relayed)
    arrived = [exchange(block, step) for step, block in enumerate(blocks)]
    for step, block in enumerate(arrived):
        result = collect([block], (step,), result)
    return result


def solution(mesh):
    return jax.shard_map(
        per_device,
        mesh=mesh,
        in_specs=(
            P(("line", "freq", "section"), "rcv", None),
            P(("line", "freq", "section"), None),
            P(("line", "freq", "section"), "rcv"),
            P(("line", "freq", "section"), "rcv"),
        ),
        out_specs=P(None, ("freq", "section"), "line", "rcv"),
        check_vma=False,
    )
```
